256 devices in a mesh: dp: 8 (over y, core), expert: 32 (over z, x).
Axes of the slice: x: 4, y: 4, z: 8, core: 2. Of those that a mesh axis runs over, the one named last changes fastest.
Arguments:
- route_experts: int32 [32768, 8], P(('dp', 'expert')), may hold values from 0 to 255, all different within a row; in each aligned block of 128 rows (0 to 127, 128 to 255, ...) at most 5 rows name the same one
- router_gate_weight: float32 [32768, 8], P(('dp', 'expert')), may hold values from 0.02 to 0.3
- forget_mask: int32 [32768], P(('dp', 'expert')), may hold values 0 or 1
- retain_mask: int32 [32768], P(('dp', 'expert')), may hold values 0 or 1
- layer_output: bfloat16 [32768, 3584], P(('dp', 'expert')), may hold values from -6 to 6
- frozen_output: bfloat16 [32768, 3584], P(('dp', 'expert')), may hold values from -6 to 6
- control_vector: float32 [3584], replicated, may hold values from 0.1 to 1
- saved_hidden: bfloat16 [2048, 160, 2048], P(('dp', 'expert')), may hold values from -6 to 6
- adapter_in: bfloat16 [2048, 16384], P('dp', 'expert'), may hold values from -0.125 to 0.125
- adapter_out: bfloat16 [3584, 16384], P('dp', 'expert'), may hold values from -0.09375 to 0.09375
Outputs:
- grad_in: float32 [2048, 16384], P('dp', 'expert')
- grad_out: float32 [3584, 16384], P('dp', 'expert')
The draws below stay inside these ranges and needn't reach their ends.
Inputs may be any that keep to these rules, and one draw needn't show every extreme that they name: `route_experts`: each row names 8 different experts; within the 128 rows of one device no expert is named more than 5 times, a bound that some block reaches.
All inputs are finite; a program needn't handle non-finite values. No bound on the sum of `forget_mask` or of `retain_mask` on one device may be relied on, other than what follows from the above.
Results may differ from the reference program's by a relative error of at most 0.0041.
Values may be sent and summed in bfloat16 or wider, within the bound.
No kernel may reach another device: no remote copies, remote signals or barrier semaphores. Data moves between devices by JAX's collectives and lax.ppermute only.
A program may use at most 128 MiB of HBM per device.

```python
import math
import jax
import jax.numpy as jnp
import numpy as np
from jax import lax

OUTPUT_FEATURES = 3584
FF = 2048
RANK = 64
TOP = 8
TOK_DEV = 128
EXPERTS = 256
CAP = 5
SLOTS = 160
TOKENS = 32768
N_DP = 8
N_EXPERT = 32


def place_ends(values, stream_key, low, top_value):
    place = [jax.random.randint(jax.random.fold_in(stream_key, axis), (), 0, length) for axis, length in enumerate(values.shape)]
    longest = values.shape.index(max(values.shape))
    next_to = place[:longest] + [(place[longest] + 1) % values.shape[longest]] + place[longest + 1:]
    return values.at[tuple(place)].set(low).at[tuple(next_to)].set(top_value)


def shard_levels(rng, dims, split, least, largest):
    loudness, own = 1.0, jax.random.fold_in(rng, 6)
    for dim, parts in split:
        draws = jnp.exp(jax.random.uniform(jax.random.fold_in(own, dim), (parts,), jnp.float32, least / len(split), largest / len(split)))
        loudness = loudness * jnp.repeat(draws, dims[dim] // parts).reshape([-1 if axis == dim else 1 for axis in range(len(dims))])
    return loudness


def routed_block(own_key, own, number, rows, number_of, top, reach, skew):
    sequence = jax.random.permutation(own_key, number_of)
    crowded, ordinary = load_shares(number_of, rows * top, reach, skew, True), load_shares(number_of, rows * top, reach, skew, False)
    places = jnp.arange(number_of)

    def named(lengths, rotation):
        used = int((lengths > 0).sum())
        fixed = max(1, used // 4)
        moved = fixed + (places - fixed + rotation * (used - fixed)) % max(1, number_of - fixed)
        return jnp.zeros((number_of,), jnp.int32).at[sequence[jnp.where(places < fixed, places, moved)]].set(jnp.asarray(lengths, jnp.int32))

    lengths = jnp.where(number % 4 == 0, named(crowded, number // 4), named(ordinary, number - number // 4 - 1))
    mixed = jax.random.permutation(jax.random.fold_in(own, 3), number_of)
    donor, receiver = mixed[0:number_of // 2 * 2:2], mixed[1:number_of // 2 * 2:2]
    slack = jnp.minimum(lengths[donor] - 1, reach - lengths[receiver]) // 2
    slack = jnp.where((donor == sequence[0]) | (receiver == sequence[0]) | (lengths[receiver] == 0), 0, jnp.maximum(slack, 0))
    moved = jax.random.randint(jax.random.fold_in(own, 4), (number_of // 2,), 0, 1 << 20) % (slack + 1)
    lengths = lengths.at[donor].add(-moved).at[receiver].add(moved)
    items = jnp.searchsorted(jnp.cumsum(lengths), jnp.arange(rows * top), side="right").astype(jnp.int32)
    grid = items.reshape(top, rows).T
    grid = grid[jax.random.permutation(jax.random.fold_in(own, 1), rows)]
    rotation = jax.random.randint(jax.random.fold_in(own, 2), (rows, 1), 0, top)
    return jnp.take_along_axis(grid, (jnp.arange(top)[None, :] + rotation) % top, axis=1)


def load_shares(count, total, most, slope, full):
    weights = [(1 << 20) // math.isqrt(grade ** slope) + 1 for grade in range(1, count + 1)]
    largest = most if full else min(most, max(-(-total // count), total * weights[0] // sum(weights)))
    least = 1 if total - largest >= count - 1 else 0
    given, spare = [largest] + [least] * (count - 1), total - largest - least * (count - 1)
    while spare > 0:
        free = [i for i in range(1, count) if given[i] < largest] or [i for i in range(1, count) if given[i] < most]
        mass, left = sum([weights[i] for i in free]), spare
        for i in free:
            extra = min(most - given[i], max(1, left * weights[i] // mass), spare)
            given[i] = given[i] + extra
            spare = spare - extra
    return np.array(given)


def scatter_about(rng, extent, deviation, bound, cuts=(), kind=jnp.bfloat16):
    factor_of = shard_levels(rng, extent, cuts, -0.22, 0.18) if cuts else 1.0
    entries = jax.random.normal(rng, extent, jnp.float32) * deviation * factor_of
    return jnp.minimum(jnp.maximum(entries, -bound), bound).astype(kind)


def setup_inputs(seed: int = 0) -> dict:
    key_list = jax.random.split(jax.random.key(seed), 11)
    route_experts_keys = jax.random.split(jax.random.fold_in(key_list[0], 1), TOKENS // TOK_DEV)
    route_experts_turns = jax.random.permutation(jax.random.fold_in(key_list[0], 3), TOKENS // TOK_DEV)
    route_experts = jax.vmap(lambda own, number: routed_block(jax.random.fold_in(key_list[0], 2), own, number, TOK_DEV, EXPERTS, TOP, CAP, 2))(route_experts_keys, route_experts_turns).reshape((TOKENS, TOP))
    router_gate_weight = jnp.clip(0.02 + 0.28 * jax.random.uniform(key_list[1], (TOKENS, TOP), jnp.float32) ** shard_levels(key_list[1], (TOKENS, TOP), ((0, 256),), -0.2, 0.2), 0.02, 0.3)
    forget_mask = place_ends((jax.random.randint(key_list[2], (TOKENS,), 0, 2) < 1).astype(jnp.int32), jax.random.fold_in(key_list[2], 1), 0, 1)
    retain_mask = place_ends((jax.random.randint(key_list[3], (TOKENS,), 0, 2) < 1).astype(jnp.int32), jax.random.fold_in(key_list[3], 1), 0, 1)
    layer_output = scatter_about(key_list[4], (TOKENS, OUTPUT_FEATURES), 1.0, 6.0, ((0, 256),))
    frozen_output = scatter_about(key_list[5], (TOKENS, OUTPUT_FEATURES), 1.0, 6.0, ((0, 256),))
    control_vector = jnp.clip(jax.random.uniform(key_list[6], (OUTPUT_FEATURES,), jnp.float32, 0.1, 1.0), 0.1, 1.0)
    saved_hidden = scatter_about(key_list[7], (N_DP * EXPERTS, SLOTS, FF), 1.0, 6.0, ((0, 256),))
    adapter_in = scatter_about(key_list[8], (FF, EXPERTS * RANK), FF ** -0.5, 0.125, ((0, 8), (1, 32)))
    adapter_out = scatter_about(key_list[9], (OUTPUT_FEATURES, EXPERTS * RANK), OUTPUT_FEATURES ** -0.5, 0.09375, ((0, 8), (1, 32)))
    return dict(route_experts=route_experts, router_gate_weight=router_gate_weight, forget_mask=forget_mask, retain_mask=retain_mask, layer_output=layer_output, frozen_output=frozen_output, control_vector=control_vector, saved_hidden=saved_hidden, adapter_in=adapter_in, adapter_out=adapter_out)


steer_coef = 20.0
retain_weight = 1.5
adapter_scale_factor = 2.0
grad_coef = 0.0625

def route_slots(experts_flat, count_all, capacity):
    onehot = (experts_flat[:, None] == jnp.arange(count_all, dtype=jnp.int32)[None, :]).astype(jnp.int32)
    running = jnp.cumsum(onehot, axis=0) - 1
    within = lax.optimization_barrier(jnp.sum(onehot * running, axis=1))
    return (experts_flat * capacity + within).astype(jnp.int32)

def token_cotangent(layer_output, frozen_output, forget_mask, retain_mask, control_vector):
    unit = control_vector / jnp.sqrt(jnp.sum(control_vector * control_vector))
    current = layer_output.astype(jnp.float32)
    forget_term = current - steer_coef * unit[None, :]
    retain_term = current - frozen_output.astype(jnp.float32)
    forget_weight = forget_mask.astype(jnp.float32)[:, None]
    retain_part = retain_mask.astype(jnp.float32)[:, None]
    return grad_coef * (forget_weight * forget_term + retain_weight * retain_part * retain_term)

def reference(route_experts, router_gate_weight, forget_mask, retain_mask, layer_output, frozen_output, control_vector, saved_hidden, adapter_in, adapter_out):
    input_adapter_factor = adapter_in.astype(jnp.float32).reshape(FF, EXPERTS, RANK)
    factor_out = adapter_out.astype(jnp.float32).reshape(OUTPUT_FEATURES, EXPERTS, RANK)

    def visit(carry, block):
        grad_in, grad_out = carry
        row_dp = (block // N_EXPERT).astype(jnp.int32)
        row_ex = (block % N_EXPERT).astype(jnp.int32)
        first = (block * TOK_DEV).astype(jnp.int32)
        experts_flat = lax.dynamic_slice_in_dim(route_experts, first, TOK_DEV, 0).reshape(-1)
        gate_block_slice = lax.dynamic_slice_in_dim(router_gate_weight, first, TOK_DEV, 0)
        output_gradient = token_cotangent(lax.dynamic_slice_in_dim(layer_output, first, TOK_DEV, 0), lax.dynamic_slice_in_dim(frozen_output, first, TOK_DEV, 0), lax.dynamic_slice_in_dim(forget_mask, first, TOK_DEV, 0), lax.dynamic_slice_in_dim(retain_mask, first, TOK_DEV, 0), control_vector)
        value_rows = (gate_block_slice[:, :, None] * adapter_scale_factor * output_gradient[:, None, :]).reshape(-1, OUTPUT_FEATURES).astype(jnp.bfloat16)
        expert_slot_index = route_slots(experts_flat, EXPERTS, CAP)
        cube = jnp.zeros((EXPERTS * CAP, OUTPUT_FEATURES), jnp.bfloat16).at[expert_slot_index].set(value_rows).reshape(EXPERTS, CAP, OUTPUT_FEATURES)
        zero_index = jnp.zeros((), jnp.int32)
        hidden = lax.dynamic_slice(saved_hidden, (row_dp * EXPERTS, row_ex * CAP, zero_index), (EXPERTS, CAP, FF))
        hidden_wide = hidden.astype(jnp.float32)
        cube_wide = cube.astype(jnp.float32)
        codes = jnp.einsum('esf,fer->esr', hidden_wide, input_adapter_factor).astype(jnp.bfloat16)
        back = jnp.einsum('esd,der->esr', cube_wide, factor_out).astype(jnp.bfloat16)
        grad_in = grad_in + jnp.einsum('esf,esr->fer', hidden_wide, back.astype(jnp.float32))
        grad_out = grad_out + jnp.einsum('esd,esr->der', cube_wide, codes.astype(jnp.float32))
        return ((grad_in, grad_out), None)
    start = (jnp.zeros((FF, EXPERTS, RANK), jnp.float32), jnp.zeros((OUTPUT_FEATURES, EXPERTS, RANK), jnp.float32))
    blocks = jnp.arange(N_DP * N_EXPERT, dtype=jnp.int32)
    (grad_in, grad_out), unused = lax.scan(visit, start, blocks)
    return (grad_in.reshape(FF, EXPERTS * RANK), grad_out.reshape(OUTPUT_FEATURES, EXPERTS * RANK))
```

```python
import functools

import jax
import jax.numpy as jnp
from jax import lax
from jax.experimental import pallas as pl
from jax.experimental.pallas import tpu as pltpu
from jax.sharding import Mesh
from jax.sharding import PartitionSpec as P

steer_coef = 20.0
retain_weight = 1.5
adapter_scale_factor = 2.0
grad_coef = 0.0625

CAP = 5
PADC = 8
VMEM_LIMIT = 60000 * 1024


def token_cotangent(layer_output, frozen_output, forget_mask, retain_mask, control_vector):
    unit = control_vector / jnp.sqrt(jnp.sum(control_vector * control_vector))
    current = layer_output.astype(jnp.float32)
    forget_term = current - steer_coef * unit[None, :]
    retain_term = current - frozen_output.astype(jnp.float32)
    forget_weight = forget_mask.astype(jnp.float32)[:, None]
    retain_part = retain_mask.astype(jnp.float32)[:, None]
    return grad_coef * (forget_weight * forget_term + retain_weight * retain_part * retain_term)


def slot_tables(route_experts, gate, experts_all):
    tokens = route_experts.shape[0]
    hit = route_experts[:, :, None] == jnp.arange(experts_all, dtype=jnp.int32)[None, None, :]
    named = jnp.any(hit, axis=1)
    weight = jnp.sum(jnp.where(hit, gate[:, :, None], 0.0), axis=1)
    row = lax.broadcasted_iota(jnp.int32, (tokens, tokens), 0)
    col = lax.broadcasted_iota(jnp.int32, (tokens, tokens), 1)
    before = (col < row).astype(jnp.bfloat16)
    rank = jnp.dot(before, named.astype(jnp.bfloat16), preferred_element_type=jnp.float32)
    slot = jnp.arange(CAP, dtype=jnp.float32)[:, None, None]
    taken = jnp.logical_and(named[None], rank[None] == slot)
    number = jnp.arange(1, tokens + 1, dtype=jnp.float32)[None, :, None]
    token = jnp.sum(jnp.where(taken, number, 0.0), axis=1) - 1.0
    weights = jnp.sum(jnp.where(taken, weight[None], 0.0), axis=1)
    return token, weights


def low_lanes(shape):
    return lax.broadcasted_iota(jnp.int32, shape, 1) < shape[1] // 2


def codes_kernel(hidden_ref, factor_ref, out_ref):
    factor = factor_ref[...]
    first = jnp.dot(hidden_ref[0], factor, preferred_element_type=jnp.float32)
    second = jnp.dot(hidden_ref[1], factor, preferred_element_type=jnp.float32)
    out_ref[...] = jnp.where(low_lanes(first.shape), first, second)


def codes_call(hidden, factor):
    experts, slots, width = hidden.shape
    columns = factor.shape[1]
    pair = 2 * columns // experts
    return pl.pallas_call(
        codes_kernel,
        grid=(experts // 2,),
        in_specs=[
            pl.BlockSpec((2, slots, width), lambda i: (i, 0, 0)),
            pl.BlockSpec((width, pair), lambda i: (0, i)),
        ],
        out_specs=pl.BlockSpec((slots, pair), lambda i: (0, i)),
        out_shape=jax.ShapeDtypeStruct((slots, columns), jnp.float32),
        cost_estimate=pl.CostEstimate(
            flops=2 * slots * width * columns * 2,
            bytes_accessed=2 * hidden.size + 2 * factor.size,
            transcendentals=0,
        ),
        name="codes",
    )(hidden, factor)


def grad_in_kernel(hidden_ref, back_ref, out_ref):
    back = back_ref[...]
    dims = (((0,), (0,)), ((), ()))
    first = lax.dot_general(hidden_ref[0], back, dims, preferred_element_type=jnp.float32)
    second = lax.dot_general(hidden_ref[1], back, dims, preferred_element_type=jnp.float32)
    out_ref[...] = jnp.where(low_lanes(first.shape), first, second)


def grad_in_call(hidden, back):
    experts, slots, width = hidden.shape
    columns = back.shape[1]
    pair = 2 * columns // experts
    return pl.pallas_call(
        grad_in_kernel,
        grid=(experts // 2,),
        in_specs=[
            pl.BlockSpec((2, slots, width), lambda i: (i, 0, 0)),
            pl.BlockSpec((slots, pair), lambda i: (0, i)),
        ],
        out_specs=pl.BlockSpec((width, pair), lambda i: (0, i)),
        out_shape=jax.ShapeDtypeStruct((width, columns), jnp.float32),
        cost_estimate=pl.CostEstimate(
            flops=2 * slots * width * columns * 2,
            bytes_accessed=2 * hidden.size + 4 * width * columns,
            transcendentals=0,
        ),
        name="grad_in",
    )(hidden, back)


def expert_kernel(index_ref, token_ref, factor_ref, codes_ref, back_ref, grad_ref, slot_ref):
    pairs = index_ref.shape[1]
    rows = index_ref.shape[2]
    experts = slot_ref.shape[0]
    step = rows // experts
    depth = token_ref.shape[1]
    lanes = 2 * (codes_ref.shape[2] // experts)
    dims = (((0,), (0,)), ((), ()))
    position = lax.broadcasted_iota(jnp.int32, (depth, rows), 0)

    def dispatch(n, carry):
        chosen = index_ref[0, pl.ds(n, 1), :]
        pick = (position == chosen).astype(jnp.float32).astype(jnp.bfloat16)
        value = lax.dot_general(pick, token_ref[n], dims, preferred_element_type=jnp.float32)
        value = value.astype(jnp.bfloat16)
        start = pl.multiple_of(n * step, step)
        for e in range(experts):
            slot_ref[e, pl.ds(start, step), :] = value[e * step : (e + 1) * step]
        return carry

    lax.fori_loop(0, pairs, dispatch, 0)
    blocks, _, quarter, _ = factor_ref.shape
    for g in range(experts // 2):
        at = slice(g * lanes, (g + 1) * lanes)
        factor = factor_ref[:, 0, :, at].reshape(blocks * quarter, lanes)
        codes = codes_ref[0, :, at]
        first = jnp.dot(slot_ref[2 * g], factor, preferred_element_type=jnp.float32)
        second = jnp.dot(slot_ref[2 * g + 1], factor, preferred_element_type=jnp.float32)
        back_ref[0, :, at] = jnp.where(low_lanes(first.shape), first, second)
        first = lax.dot_general(slot_ref[2 * g], codes, dims, preferred_element_type=jnp.float32)
        second = lax.dot_general(
            slot_ref[2 * g + 1], codes, dims, preferred_element_type=jnp.float32
        )
        grad = jnp.where(low_lanes(first.shape), first, second)
        grad_ref[:, 0, :, at] = grad.reshape(blocks, quarter, lanes)


def expert_call(index, tokens, factor, codes, experts):
    groups, pairs, rows = index.shape
    _, depth, width = tokens.shape
    blocks, _, quarter, columns = factor.shape
    slots = codes.shape[1]
    return pl.pallas_call(
        expert_kernel,
        grid=(groups,),
        in_specs=[
            pl.BlockSpec((1, pairs, rows), lambda i: (i, 0, 0)),
            pl.BlockSpec((pairs, depth, width), lambda i: (0, 0, 0)),
            pl.BlockSpec((blocks, 1, quarter, columns), lambda i: (0, i, 0, 0)),
            pl.BlockSpec((1, slots, columns), lambda i: (i, 0, 0)),
        ],
        out_specs=[
            pl.BlockSpec((1, slots, columns), lambda i: (i, 0, 0)),
            pl.BlockSpec((blocks, 1, quarter, columns), lambda i: (0, i, 0, 0)),
        ],
        out_shape=[
            jax.ShapeDtypeStruct((groups, slots, columns), jnp.float32),
            jax.ShapeDtypeStruct((blocks, groups, quarter, columns), jnp.float32),
        ],
        scratch_shapes=[pltpu.VMEM((experts, slots, width), jnp.bfloat16)],
        compiler_params=pltpu.CompilerParams(vmem_limit_bytes=VMEM_LIMIT),
        cost_estimate=pl.CostEstimate(
            flops=groups * 2 * (pairs * rows * depth * width + 4 * slots * width * columns),
            bytes_accessed=2 * tokens.size + 6 * factor.size + 6 * codes.size,
            transcendentals=0,
        ),
        name="experts",
    )(index, tokens, factor, codes)


def local(
    route_experts,
    router_gate_weight,
    forget_mask,
    retain_mask,
    layer_output,
    frozen_output,
    control_vector,
    saved_hidden,
    adapter_in,
    adapter_out,
):
    experts, slot_count, _ = saved_hidden.shape
    tokens, features = layer_output.shape
    columns = adapter_in.shape[1]
    rank = columns // experts
    zs, xs = lax.axis_size("z"), lax.axis_size("x")
    dps = lax.axis_size("y") * lax.axis_size("c")
    blocks = zs * xs
    quarter = features // (dps * xs)
    width = features // xs

    gathered_in = lax.all_gather(adapter_in, ("y", "c"), axis=0, tiled=True)

    cotangent = token_cotangent(
        layer_output, frozen_output, forget_mask, retain_mask, control_vector
    ).astype(jnp.bfloat16)
    parts = cotangent.reshape(tokens, dps, xs, quarter).transpose(2, 0, 1, 3)
    mine = lax.all_to_all(parts.reshape(xs * tokens, width), "x", 0, 0, tiled=True)
    everyone = lax.all_gather(mine, "z", axis=0, tiled=True)

    token, weights = slot_tables(route_experts, router_gate_weight, blocks * experts)
    token = token.reshape(CAP, zs, 1, xs * experts).transpose(1, 2, 0, 3)
    token = jnp.broadcast_to(token, (zs, xs, CAP, xs * experts))
    weights = weights.reshape(CAP, zs, xs, experts).transpose(1, 2, 0, 3)
    table = jnp.concatenate([token, weights], axis=3)
    table = jnp.pad(
        table,
        ((0, 0), (0, 0), (0, PADC - CAP), (0, 128 - table.shape[3])),
        constant_values=-1.0,
    )
    table = lax.all_to_all(table.reshape(blocks * PADC, 128), ("z", "x"), 0, 0, tiled=True)
    table = table.reshape(blocks, PADC, 128)
    scale = adapter_scale_factor * table[:, :CAP, xs * experts : (xs + 1) * experts]
    scale = scale.reshape(slot_count, experts, 1)
    index = table[:, :, : xs * experts].astype(jnp.int32)
    index = index.reshape(blocks // 2, 2, PADC, xs, experts)
    odd = jnp.arange(2, dtype=jnp.int32).reshape(1, 2, 1, 1, 1) * tokens
    index = jnp.where(index >= 0, index + odd, -1)
    index = index.transpose(3, 0, 4, 1, 2).reshape(xs, blocks // 2, experts * 2 * PADC)

    factor = lax.all_to_all(adapter_out, "x", 0, 0, tiled=True)
    factor = jnp.broadcast_to(factor[None], (dps,) + factor.shape)
    factor = lax.all_to_all(factor, ("y", "c"), 0, 0, tiled=True)
    factor = factor.reshape(dps, xs, quarter, columns)

    codes = codes_call(saved_hidden, gathered_in)
    codes = lax.reduce_precision(codes, 8, 7).reshape(slot_count, experts, rank)
    codes = (codes * scale).reshape(blocks, CAP, columns)
    codes = jnp.pad(codes, ((0, 0), (0, PADC - CAP), (0, 0))).astype(jnp.bfloat16)
    codes = codes.reshape(1, blocks * PADC, columns)
    codes = jnp.broadcast_to(codes, (xs, blocks * PADC, columns))
    codes = lax.all_to_all(codes, "x", 0, 0, tiled=True)

    back, grad_out = expert_call(
        index,
        everyone.reshape(blocks // 2, 2 * tokens, width),
        factor,
        codes,
        experts,
    )
    grad_out = lax.psum_scatter(
        grad_out.reshape(dps * xs * quarter, columns),
        ("y", "c"),
        scatter_dimension=0,
        tiled=True,
    )
    back = lax.all_to_all(back, "x", 0, 0, tiled=True)
    back = jnp.sum(back, axis=0).reshape(blocks, PADC, columns)[:, :CAP]
    back = (back.reshape(slot_count, experts, rank) * scale).astype(jnp.bfloat16)
    grad_in = grad_in_call(saved_hidden, back.reshape(slot_count, columns))
    grad_in = lax.psum_scatter(grad_in, ("y", "c"), scatter_dimension=0, tiled=True)
    grad_out = lax.all_to_all(grad_out, "x", 0, 0, tiled=True)
    return (grad_in, grad_out)


def solution(mesh):
    dps, blocks = mesh.devices.shape
    xs = 4 if blocks >= 32 else 2
    cores = 2
    fine = Mesh(
        mesh.devices.reshape(dps // cores, cores, blocks // xs, xs), ("y", "c", "z", "x")
    )
    dp, ep = ("y", "c"), ("z", "x")
    return jax.shard_map(
        local,
        mesh=fine,
        in_specs=(
            P(dp + ep, None),
            P(dp + ep, None),
            P(dp + ep),
            P(dp + ep),
            P(dp + ep, None),
            P(dp + ep, None),
            P(),
            P(dp + ep, None, None),
            P(dp, ep),
            P(dp, ep),
        ),
        out_specs=(P(dp, ep), P(dp, ep)),
        check_vma=False,
    )
```

```python
import functools

import jax
import jax.numpy as jnp
from jax import lax
from jax.experimental import pallas as pl
from jax.experimental.pallas import tpu as pltpu
from jax.sharding import Mesh
from jax.sharding import PartitionSpec as P


steer_coef = 20.0
retain_weight = 1.5
adapter_scale_factor = 2.0
grad_coef = 0.0625

CAP = 5
PADC = 8
VMEM_LIMIT = 58 * 1024 * 1024


def token_cotangent(layer_output, frozen_output, forget_mask, retain_mask, control_vector):
    unit = control_vector / jnp.sqrt(jnp.sum(control_vector * control_vector))
    current = layer_output.astype(jnp.float32)
    forget_term = current - steer_coef * unit[None, :]
    retain_term = current - frozen_output.astype(jnp.float32)
    forget_weight = forget_mask.astype(jnp.float32)[:, None]
    retain_part = retain_mask.astype(jnp.float32)[:, None]
    return grad_coef * (forget_weight * forget_term + retain_weight * retain_part * retain_term)


def slot_tables(route_experts, gate, experts_all):
    tokens = route_experts.shape[0]
    hit = route_experts[:, :, None] == jnp.arange(experts_all, dtype=jnp.int32)[None, None, :]
    named = jnp.any(hit, axis=1)
    weight = jnp.sum(jnp.where(hit, gate[:, :, None], 0.0), axis=1)
    row = lax.broadcasted_iota(jnp.int32, (tokens, tokens), 0)
    col = lax.broadcasted_iota(jnp.int32, (tokens, tokens), 1)
    before = (col < row).astype(jnp.bfloat16)
    rank = jnp.dot(before, named.astype(jnp.bfloat16), preferred_element_type=jnp.float32)
    slot = jnp.arange(CAP, dtype=jnp.float32)[:, None, None]
    taken = jnp.logical_and(named[None], rank[None] == slot)
    number = jnp.arange(1, tokens + 1, dtype=jnp.float32)[None, :, None]
    token = jnp.sum(jnp.where(taken, number, 0.0), axis=1) - 1.0
    weights = jnp.sum(jnp.where(taken, weight[None], 0.0), axis=1)
    return token, weights


def low_lanes(shape):
    return lax.broadcasted_iota(jnp.int32, shape, 1) < shape[1] // 2


def codes_kernel(hidden_ref, factor_ref, out_ref):
    factor = factor_ref[...]
    first = jnp.dot(hidden_ref[0], factor, preferred_element_type=jnp.float32)
    second = jnp.dot(hidden_ref[1], factor, preferred_element_type=jnp.float32)
    out_ref[...] = jnp.where(low_lanes(first.shape), first, second)


def codes_call(hidden, factor):
    experts, slots, width = hidden.shape
    columns = factor.shape[1]
    pair = 2 * columns // experts
    return pl.pallas_call(
        codes_kernel,
        grid=(experts // 2,),
        in_specs=[
            pl.BlockSpec((2, slots, width), lambda i: (i, 0, 0)),
            pl.BlockSpec((width, pair), lambda i: (0, i)),
        ],
        out_specs=pl.BlockSpec((slots, pair), lambda i: (0, i)),
        out_shape=jax.ShapeDtypeStruct((slots, columns), jnp.float32),
        cost_estimate=pl.CostEstimate(
            flops=2 * slots * width * columns * 2,
            bytes_accessed=2 * hidden.size + 2 * factor.size,
            transcendentals=0,
        ),
        name="codes",
    )(hidden, factor)


def grad_in_kernel(core_ref, hidden_ref, pick_ref, scale_ref, *refs):
    part_refs, (mine_ref, theirs_ref) = refs[:-2], refs[-2:]
    sums = []
    for part_ref in part_refs:
        total = part_ref[0]
        for n in range(1, part_ref.shape[0]):
            total = total + part_ref[n]
        sums.append(total)
    back = jnp.concatenate(sums, axis=0)
    lanes = back.shape[1]

    def split(value):
        high = value.astype(jnp.bfloat16)
        low = (value - high.astype(jnp.float32)).astype(jnp.bfloat16)
        return jnp.concatenate([high, low], axis=1)

    def join(value):
        return value[:, :lanes] + value[:, lanes:]

    back = join(jnp.dot(pick_ref[...], split(back), preferred_element_type=jnp.float32))
    both = split(back * scale_ref[...])
    dims = (((0,), (0,)), ((), ()))
    first = join(lax.dot_general(hidden_ref[0], both, dims, preferred_element_type=jnp.float32))
    second = join(lax.dot_general(hidden_ref[1], both, dims, preferred_element_type=jnp.float32))
    total = jnp.where(low_lanes(first.shape), first, second)
    others, width, _ = mine_ref.shape
    first_core = core_ref[0] == 0
    for y in range(others):
        one = total[2 * y * width : (2 * y + 1) * width]
        two = total[(2 * y + 1) * width : (2 * y + 2) * width]
        mine_ref[y] = jnp.where(first_core, one, two)
        theirs_ref[y] = jnp.where(first_core, two, one)


def grad_in_call(core, hidden, pick, scale, parts, others):
    experts, slots, width = hidden.shape
    columns = scale.shape[1]
    pair = 2 * columns // experts
    share = width // (2 * others)
    return pl.pallas_call(
        grad_in_kernel,
        grid=(experts // 2,),
        in_specs=[
            pl.BlockSpec(memory_space=pltpu.SMEM),
            pl.BlockSpec((2, slots, width), lambda i: (i, 0, 0)),
            pl.BlockSpec(pick.shape, lambda i: (0, 0)),
            pl.BlockSpec((slots, pair), lambda i: (0, i)),
        ]
        + [pl.BlockSpec(p.shape[:2] + (pair,), lambda i: (0, 0, i)) for p in parts],
        out_specs=[pl.BlockSpec((others, share, pair), lambda i: (0, 0, i))] * 2,
        out_shape=[jax.ShapeDtypeStruct((others, share, columns), jnp.float32)] * 2,
        cost_estimate=pl.CostEstimate(
            flops=4 * slots * width * columns * 2,
            bytes_accessed=2 * hidden.size + 4 * width * columns,
            transcendentals=0,
        ),
        name="grad_in",
    )(core, hidden, pick, scale, *parts)


def back_kernel(starts, index_ref, *refs):
    count = len(starts)
    token_refs, (factor_ref, back_ref, slot_ref) = refs[:count], (refs[count], *refs[-2:])
    rows = index_ref.shape[2]
    _, experts, slots, width = slot_ref.shape
    step = rows // experts
    depth = sum(t.shape[0] for t in token_refs) * step // slots
    lanes = 2 * (back_ref.shape[2] // experts)
    dims = (((0,), (0,)), ((), ()))
    position = lax.broadcasted_iota(jnp.int32, (depth, rows), 0)
    base = 0
    for first_pair, token_ref in zip(starts, token_refs):

        def dispatch(n, carry, token_ref=token_ref, base=base, first_pair=first_pair):
            chosen = index_ref[0, pl.ds(first_pair + n, 1), :]
            pick = (position == chosen).astype(jnp.float32).astype(jnp.bfloat16)
            source = token_ref[pl.ds(pl.multiple_of(n * depth, depth), depth), :]
            value = lax.dot_general(pick, source, dims, preferred_element_type=jnp.float32)
            value = value.astype(jnp.bfloat16)
            start = pl.multiple_of((base + n) * step, step)
            for e in range(experts):
                slot_ref[0, e, pl.ds(start, step), :] = value[e * step : (e + 1) * step]
            return carry

        pairs = token_ref.shape[0] // depth
        lax.fori_loop(0, pairs, dispatch, 0)
        base += pairs
    blocks, _, quarter, _ = factor_ref.shape
    for g in range(experts // 2):
        at = slice(g * lanes, (g + 1) * lanes)
        factor = factor_ref[:, 0, :, at].reshape(blocks * quarter, lanes)
        both = slot_ref[0, 2 * g : 2 * g + 2].reshape(2 * slots, width)
        result = jnp.dot(both, factor, preferred_element_type=jnp.float32)
        first, second = result[:slots], result[slots:]
        back_ref[0, :, at] = jnp.where(low_lanes(first.shape), first, second)


def back_call(index, tokens, starts, factor, experts, pair_depth, all_slots, before, into):
    groups, pairs, rows = index.shape
    width = tokens[0].shape[1]
    blocks, _, quarter, columns = factor.shape
    depth = sum(t.shape[0] for t in tokens)
    slots = depth // pair_depth * rows // experts
    more = [] if into is None else [into]
    return pl.pallas_call(
        functools.partial(back_kernel, tuple(starts)),
        grid=(groups,),
        in_specs=[pl.BlockSpec((1, pairs, rows), lambda i: (i, 0, 0))]
        + [pl.BlockSpec(t.shape, lambda i: (0, 0)) for t in tokens]
        + [pl.BlockSpec((blocks, 1, quarter, columns), lambda i: (0, i, 0, 0))]
        + [pl.BlockSpec(memory_space=pl.ANY)] * len(more),
        input_output_aliases={len(tokens) + 2: 0} if more else {},
        out_specs=[
            pl.BlockSpec((1, slots, columns), lambda i: (i, before // slots, 0)),
            pl.BlockSpec((1, experts, slots, width), lambda i: (i, 0, 0, 0)),
        ],
        out_shape=[
            jax.ShapeDtypeStruct((groups, all_slots, columns), jnp.float32),
            jax.ShapeDtypeStruct((groups, experts, slots, width), jnp.bfloat16),
        ],
        compiler_params=pltpu.CompilerParams(vmem_limit_bytes=VMEM_LIMIT),
        cost_estimate=pl.CostEstimate(
            flops=groups * 2 * (rows * depth * width + 4 * slots * width * columns),
            bytes_accessed=2 * depth * width + 2 * factor.size + 4 * slots * columns * groups
            + 2 * groups * experts * slots * width,
            transcendentals=0,
        ),
        name="back",
    )(index, *tokens, factor, *more)


def grad_out_kernel(core_ref, *refs):
    slot_refs, (codes_ref, mine_ref, theirs_ref) = refs[:-3], refs[-3:]
    dims = (((0,), (0,)), ((), ()))
    codes = codes_ref[0]
    first = jnp.concatenate([s[0, 0] for s in slot_refs], axis=0)
    second = jnp.concatenate([s[0, 1] for s in slot_refs], axis=0)
    first = lax.dot_general(first, codes, dims, preferred_element_type=jnp.float32)
    second = lax.dot_general(second, codes, dims, preferred_element_type=jnp.float32)
    grad = jnp.where(low_lanes(first.shape), first, second)
    others, _, quarter, _ = mine_ref.shape
    first_core = core_ref[0] == 0
    for y in range(others):
        one = grad[2 * y * quarter : (2 * y + 1) * quarter]
        two = grad[(2 * y + 1) * quarter : (2 * y + 2) * quarter]
        mine_ref[y, 0] = jnp.where(first_core, one, two)
        theirs_ref[y, 0] = jnp.where(first_core, two, one)


def grad_out_call(core, slot_parts, codes, others, quarter):
    groups, slots, columns = codes.shape
    _, experts, _, width = slot_parts[0].shape
    pair = 2 * columns // experts
    return pl.pallas_call(
        grad_out_kernel,
        grid=(groups, experts // 2),
        in_specs=[pl.BlockSpec(memory_space=pltpu.SMEM)]
        + [
            pl.BlockSpec((1, 2, s.shape[2], width), lambda i, g: (i, g, 0, 0)) for s in slot_parts
        ]
        + [pl.BlockSpec((1, slots, pair), lambda i, g: (i, 0, g))],
        out_specs=[pl.BlockSpec((others, 1, quarter, pair), lambda i, g: (0, i, 0, g))] * 2,
        out_shape=[jax.ShapeDtypeStruct((others, groups, quarter, columns), jnp.float32)] * 2,
        compiler_params=pltpu.CompilerParams(vmem_limit_bytes=VMEM_LIMIT),
        cost_estimate=pl.CostEstimate(
            flops=groups * 4 * slots * width * columns,
            bytes_accessed=2 * groups * experts * slots * width + 4 * groups * width * columns,
            transcendentals=0,
        ),
        name="grad_out",
    )(core, *slot_parts, codes)


def turn(blocks, shift):
    count = blocks.shape[0]
    return lax.dynamic_slice_in_dim(jnp.concatenate([blocks, blocks], axis=0), shift, count, 0)


def around(mine):
    size = lax.axis_size("z")
    up = [(i, (i + 1) % size) for i in range(size)]
    down = [(i, (i - 1) % size) for i in range(size)]
    half = mine.shape[0] // 2
    groups = [[(0, mine)]]
    low = high = mine
    for k in range(1, size // 2):
        low = lax.ppermute(low, "z", up)
        high = lax.ppermute(high, "z", down)
        found = [(2 * (size - k), low), (2 * k, high)]
        if k < size // 2 - 1:
            groups[0] += found
        else:
            groups.append(found)
    k = size // 2
    low = lax.ppermute(low[:half], "z", up)
    high = lax.ppermute(high[half:], "z", down)
    groups.append([(2 * k, low), (2 * k + 1, high)])
    return groups


def local(
    route_experts,
    router_gate_weight,
    forget_mask,
    retain_mask,
    layer_output,
    frozen_output,
    control_vector,
    saved_hidden,
    adapter_in,
    adapter_out,
):
    experts, slot_count, _ = saved_hidden.shape
    tokens, features = layer_output.shape
    columns = adapter_in.shape[1]
    rank = columns // experts
    zs, xs = lax.axis_size("z"), lax.axis_size("x")
    dps = lax.axis_size("y") * lax.axis_size("c")
    blocks = zs * xs
    quarter = features // (dps * xs)
    width = features // xs

    gathered_in = lax.all_gather(adapter_in, ("y", "c"), axis=0, tiled=True)

    cotangent = token_cotangent(
        layer_output, frozen_output, forget_mask, retain_mask, control_vector
    ).astype(jnp.bfloat16)
    parts = cotangent.reshape(tokens, dps, xs, quarter).transpose(2, 0, 1, 3)
    mine = lax.all_to_all(parts.reshape(xs * tokens, width), "x", 0, 0, tiled=True)
    groups = around(mine)

    token, weights = slot_tables(route_experts, router_gate_weight, blocks * experts)
    token = token.reshape(CAP, zs, 1, xs * experts).transpose(1, 2, 0, 3)
    token = jnp.broadcast_to(token, (zs, xs, CAP, xs * experts))
    weights = weights.reshape(CAP, zs, xs, experts).transpose(1, 2, 0, 3)
    table = jnp.concatenate([token, weights], axis=3)
    table = jnp.pad(
        table,
        ((0, 0), (0, 0), (0, PADC - CAP), (0, 128 - table.shape[3])),
        constant_values=-1.0,
    )
    table = lax.all_to_all(table.reshape(blocks * PADC, 128), ("z", "x"), 0, 0, tiled=True)
    table = table.reshape(blocks, PADC, 128)
    scale = table[:, :CAP, xs * experts : (xs + 1) * experts]
    scale = adapter_scale_factor * scale
    scale = jnp.broadcast_to(
        scale.reshape(slot_count, experts, 1), (slot_count, experts, rank)
    ).reshape(slot_count, columns)
    here = lax.axis_index("z")
    index = turn(table[:, :, : xs * experts].reshape(zs, xs, PADC, xs * experts), here)
    index = index.astype(jnp.int32)
    index = index.reshape(blocks // 2, 2, PADC, xs, experts)
    odd = jnp.arange(2, dtype=jnp.int32).reshape(1, 2, 1, 1, 1) * tokens
    index = jnp.where(index >= 0, index + odd, -1)
    index = index.transpose(3, 0, 4, 1, 2).reshape(xs, blocks // 2, experts * 2 * PADC)

    factor = lax.all_to_all(adapter_out, "x", 0, 0, tiled=True)
    factor = lax.all_gather(factor, ("y", "c"), axis=0, tiled=True)
    factor = factor.reshape(dps, xs, quarter, columns)

    order = [start // 2 for group in groups for start, _ in group]
    order = list(dict.fromkeys(order))
    slot = jnp.arange(slot_count, dtype=jnp.int32)
    ahead = lax.rem(slot // (xs * CAP) - here + zs, zs)
    place = sum(jnp.where(ahead == o, n, 0) for n, o in enumerate(order))
    place = (place * xs + lax.rem(slot // CAP, xs)) * PADC + lax.rem(slot, CAP)
    pick = place[:, None] == jnp.arange(blocks * PADC, dtype=jnp.int32)[None, :]
    pick = pick.astype(jnp.bfloat16)

    codes = codes_call(saved_hidden, gathered_in)
    codes = (lax.reduce_precision(codes, 8, 7) * scale).astype(jnp.bfloat16)
    codes = lax.dot_general(
        pick, codes, (((0,), (0,)), ((), ())), preferred_element_type=jnp.float32
    )
    codes = jnp.broadcast_to(codes.astype(jnp.bfloat16)[None], (xs, blocks * PADC, columns))
    codes = lax.all_to_all(codes, "x", 0, 0, tiled=True)

    step = 2 * PADC
    sizes = [sum(t.shape[0] for _, t in g) // (2 * tokens) * step for g in groups]
    places = [(sizes[0], 0), (sizes[1] + sizes[2], 0), (sizes[1] + sizes[2], sizes[1])]
    backs, slot_parts, part = [], [], None
    for n, group in enumerate(groups):
        starts, parts = [f[0] for f in group], [f[1] for f in group]
        into = part if places[n][1] else None
        part, slots = back_call(index, parts, starts, factor, experts, 2 * tokens, *places[n], into)
        slot_parts.append(slots)
        if n != 1:
            backs.append(lax.all_to_all(part, "x", 0, 0, tiled=True))
    others = lax.axis_size("y")
    core = lax.axis_index("c").astype(jnp.int32).reshape(1)
    twins = [(0, 1), (1, 0)]
    out_mine, out_theirs = grad_out_call(core, slot_parts, codes, others, quarter)
    out_theirs = lax.ppermute(out_theirs, "c", twins)
    in_mine, in_theirs = grad_in_call(core, saved_hidden, pick, scale, backs, others)
    in_theirs = lax.ppermute(in_theirs, "c", twins)
    grad_out = (out_mine + out_theirs).astype(jnp.bfloat16)
    grad_out = grad_out.reshape(others * xs, quarter, columns)
    grad_out = lax.all_to_all(grad_out, ("y", "x"), 0, 0, tiled=True)
    grad_out = grad_out.reshape(others, xs * quarter, columns)
    grad_out = jnp.sum(grad_out.astype(jnp.float32), axis=0)
    grad_in = (in_mine + in_theirs).astype(jnp.bfloat16)
    grad_in = lax.all_to_all(grad_in, "y", 0, 0, tiled=True)
    grad_in = jnp.sum(grad_in.astype(jnp.float32), axis=0)
    return (grad_in, grad_out)


def solution(mesh):
    dps, blocks = mesh.devices.shape
    xs = 4 if blocks >= 32 else 2
    cores = 2
    fine = Mesh(
        mesh.devices.reshape(dps // cores, cores, blocks // xs, xs), ("y", "c", "z", "x")
    )
    dp, ep = ("y", "c"), ("z", "x")
    return jax.shard_map(
        local,
        mesh=fine,
        in_specs=(
            P(dp + ep, None),
            P(dp + ep, None),
            P(dp + ep),
            P(dp + ep),
            P(dp + ep, None),
            P(dp + ep, None),
            P(),
            P(dp + ep, None, None),
            P(dp, ep),
            P(dp, ep),
        ),
        out_specs=(P(dp, ep), P(dp, ep)),
        check_vma=False,
    )
```

```python
import functools

import jax
import jax.numpy as jnp
from jax import lax
from jax.experimental import pallas as pl
from jax.experimental.pallas import tpu as pltpu
from jax.sharding import Mesh
from jax.sharding import PartitionSpec as P


steer_coef = 20.0
retain_weight = 1.5
adapter_scale_factor = 2.0
grad_coef = 0.0625

CAP = 5
PADC = 8
VMEM_LIMIT = 58 * 1024 * 1024


def token_cotangent(layer_output, frozen_output, forget_mask, retain_mask, control_vector):
    unit = control_vector / jnp.sqrt(jnp.sum(control_vector * control_vector))
    current = layer_output.astype(jnp.float32)
    forget_term = current - steer_coef * unit[None, :]
    retain_term = current - frozen_output.astype(jnp.float32)
    forget_weight = forget_mask.astype(jnp.float32)[:, None]
    retain_part = retain_mask.astype(jnp.float32)[:, None]
    return grad_coef * (forget_weight * forget_term + retain_weight * retain_part * retain_term)


def slot_tables(route_experts, gate, experts_all):
    tokens = route_experts.shape[0]
    hit = route_experts[:, :, None] == jnp.arange(experts_all, dtype=jnp.int32)[None, None, :]
    named = jnp.any(hit, axis=1)
    weight = jnp.sum(jnp.where(hit, gate[:, :, None], 0.0), axis=1)
    row = lax.broadcasted_iota(jnp.int32, (tokens, tokens), 0)
    col = lax.broadcasted_iota(jnp.int32, (tokens, tokens), 1)
    before = (col < row).astype(jnp.bfloat16)
    rank = jnp.dot(before, named.astype(jnp.bfloat16), preferred_element_type=jnp.float32)
    slot = jnp.arange(CAP, dtype=jnp.float32)[:, None, None]
    taken = jnp.logical_and(named[None], rank[None] == slot)
    number = jnp.arange(1, tokens + 1, dtype=jnp.float32)[None, :, None]
    token = jnp.sum(jnp.where(taken, number, 0.0), axis=1) - 1.0
    weights = jnp.sum(jnp.where(taken, weight[None], 0.0), axis=1)
    return token, weights


def low_lanes(shape):
    return lax.broadcasted_iota(jnp.int32, shape, 1) < shape[1] // 2


def own_order(here_ref, mine, theirs, others):
    first_core = here_ref[0] == 0
    parts = []
    for y in range(others):
        at = lax.rem(y - here_ref[1] + others, others)
        one, two = mine(at), theirs(at)
        parts += [jnp.where(first_core, one, two), jnp.where(first_core, two, one)]
    return jnp.concatenate(parts, axis=0)


def codes_kernel(here_ref, hidden_ref, mine_ref, theirs_ref, out_ref):
    factor = own_order(
        here_ref, lambda at: mine_ref[at], lambda at: theirs_ref[at], mine_ref.shape[0]
    )
    first = jnp.dot(hidden_ref[0], factor, preferred_element_type=jnp.float32)
    second = jnp.dot(hidden_ref[1], factor, preferred_element_type=jnp.float32)
    out_ref[...] = jnp.where(low_lanes(first.shape), first, second)


def codes_call(here, hidden, mine, theirs):
    experts, slots, width = hidden.shape
    others, share, columns = mine.shape
    pair = 2 * columns // experts
    return pl.pallas_call(
        codes_kernel,
        grid=(experts // 2,),
        in_specs=[
            pl.BlockSpec(memory_space=pltpu.SMEM),
            pl.BlockSpec((2, slots, width), lambda i: (i, 0, 0)),
            pl.BlockSpec((others, share, pair), lambda i: (0, 0, i)),
            pl.BlockSpec((others, share, pair), lambda i: (0, 0, i)),
        ],
        out_specs=pl.BlockSpec((slots, pair), lambda i: (0, i)),
        out_shape=jax.ShapeDtypeStruct((slots, columns), jnp.float32),
        cost_estimate=pl.CostEstimate(
            flops=2 * slots * width * columns * 2,
            bytes_accessed=2 * hidden.size + 4 * mine.size,
            transcendentals=0,
        ),
        name="codes",
    )(here, hidden, mine, theirs)


def grad_in_kernel(core_ref, hidden_ref, pick_ref, scale_ref, *refs):
    part_refs, (mine_ref, theirs_ref) = refs[:-2], refs[-2:]
    sums = []
    for part_ref in part_refs:
        total = part_ref[0]
        for n in range(1, part_ref.shape[0]):
            total = total + part_ref[n]
        sums.append(total)
    back = jnp.concatenate(sums, axis=0)
    lanes = back.shape[1]

    def split(value):
        high = value.astype(jnp.bfloat16)
        low = (value - high.astype(jnp.float32)).astype(jnp.bfloat16)
        return jnp.concatenate([high, low], axis=1)

    def join(value):
        return value[:, :lanes] + value[:, lanes:]

    back = join(jnp.dot(pick_ref[...], split(back), preferred_element_type=jnp.float32))
    both = split(back * scale_ref[...])
    dims = (((0,), (0,)), ((), ()))
    first = join(lax.dot_general(hidden_ref[0], both, dims, preferred_element_type=jnp.float32))
    second = join(lax.dot_general(hidden_ref[1], both, dims, preferred_element_type=jnp.float32))
    total = jnp.where(low_lanes(first.shape), first, second)
    others, width, _ = mine_ref.shape
    first_core = core_ref[0] == 0
    for y in range(others):
        one = total[2 * y * width : (2 * y + 1) * width]
        two = total[(2 * y + 1) * width : (2 * y + 2) * width]
        at = lax.rem(y - core_ref[1] + others, others)
        mine_ref[at] = jnp.where(first_core, one, two)
        theirs_ref[at] = jnp.where(first_core, two, one)


def grad_in_call(core, hidden, pick, scale, parts, others):
    experts, slots, width = hidden.shape
    columns = scale.shape[1]
    pair = 2 * columns // experts
    share = width // (2 * others)
    return pl.pallas_call(
        grad_in_kernel,
        grid=(experts // 2,),
        in_specs=[
            pl.BlockSpec(memory_space=pltpu.SMEM),
            pl.BlockSpec((2, slots, width), lambda i: (i, 0, 0)),
            pl.BlockSpec(pick.shape, lambda i: (0, 0)),
            pl.BlockSpec((slots, pair), lambda i: (0, i)),
        ]
        + [pl.BlockSpec(p.shape[:2] + (pair,), lambda i: (0, 0, i)) for p in parts],
        out_specs=[pl.BlockSpec((others, share, pair), lambda i: (0, 0, i))] * 2,
        out_shape=[jax.ShapeDtypeStruct((others, share, columns), jnp.float32)] * 2,
        cost_estimate=pl.CostEstimate(
            flops=4 * slots * width * columns * 2,
            bytes_accessed=2 * hidden.size + 4 * width * columns,
            transcendentals=0,
        ),
        name="grad_in",
    )(core, hidden, pick, scale, *parts)


def back_kernel(starts, here_ref, index_ref, *refs):
    count = len(starts)
    token_refs, (mine_ref, theirs_ref) = refs[:count], refs[count : count + 2]
    back_ref, slot_ref = refs[-2:]
    rows = index_ref.shape[2]
    _, experts, slots, width = slot_ref.shape
    step = rows // experts
    depth = sum(t.shape[0] for t in token_refs) * step // slots
    lanes = 2 * (back_ref.shape[2] // experts)
    dims = (((0,), (0,)), ((), ()))
    position = lax.broadcasted_iota(jnp.int32, (depth, rows), 0)
    base = 0
    for first_pair, token_ref in zip(starts, token_refs):

        def dispatch(n, carry, token_ref=token_ref, base=base, first_pair=first_pair):
            chosen = index_ref[0, pl.ds(first_pair + n, 1), :]
            pick = (position == chosen).astype(jnp.float32).astype(jnp.bfloat16)
            source = token_ref[pl.ds(pl.multiple_of(n * depth, depth), depth), :]
            value = lax.dot_general(pick, source, dims, preferred_element_type=jnp.float32)
            value = value.astype(jnp.bfloat16)
            start = pl.multiple_of((base + n) * step, step)
            for e in range(experts):
                slot_ref[0, e, pl.ds(start, step), :] = value[e * step : (e + 1) * step]
            return carry

        pairs = token_ref.shape[0] // depth
        lax.fori_loop(0, pairs, dispatch, 0)
        base += pairs
    for g in range(experts // 2):
        at = slice(g * lanes, (g + 1) * lanes)
        factor = own_order(
            here_ref,
            lambda n, at=at: mine_ref[n, 0, :, at],
            lambda n, at=at: theirs_ref[n, 0, :, at],
            mine_ref.shape[0],
        )
        both = slot_ref[0, 2 * g : 2 * g + 2].reshape(2 * slots, width)
        result = jnp.dot(both, factor, preferred_element_type=jnp.float32)
        first, second = result[:slots], result[slots:]
        back_ref[0, :, at] = jnp.where(low_lanes(first.shape), first, second)


def back_call(here, index, tokens, starts, factor, experts, pair_depth, all_slots, before, into):
    groups, pairs, rows = index.shape
    width = tokens[0].shape[1]
    others, _, quarter, columns = factor[0].shape
    depth = sum(t.shape[0] for t in tokens)
    slots = depth // pair_depth * rows // experts
    more = [] if into is None else [into]
    return pl.pallas_call(
        functools.partial(back_kernel, tuple(starts)),
        grid=(groups,),
        in_specs=[pl.BlockSpec(memory_space=pltpu.SMEM)]
        + [pl.BlockSpec((1, pairs, rows), lambda i: (i, 0, 0))]
        + [pl.BlockSpec(t.shape, lambda i: (0, 0)) for t in tokens]
        + [pl.BlockSpec((others, 1, quarter, columns), lambda i: (0, i, 0, 0))] * 2
        + [pl.BlockSpec(memory_space=pl.ANY)] * len(more),
        input_output_aliases={len(tokens) + 4: 0} if more else {},
        out_specs=[
            pl.BlockSpec((1, slots, columns), lambda i: (i, before // slots, 0)),
            pl.BlockSpec((1, experts, slots, width), lambda i: (i, 0, 0, 0)),
        ],
        out_shape=[
            jax.ShapeDtypeStruct((groups, all_slots, columns), jnp.float32),
            jax.ShapeDtypeStruct((groups, experts, slots, width), jnp.bfloat16),
        ],
        compiler_params=pltpu.CompilerParams(vmem_limit_bytes=VMEM_LIMIT),
        cost_estimate=pl.CostEstimate(
            flops=groups * 2 * (rows * depth * width + 4 * slots * width * columns),
            bytes_accessed=2 * depth * width + 4 * factor[0].size + 4 * slots * columns * groups
            + 2 * groups * experts * slots * width,
            transcendentals=0,
        ),
        name="back",
    )(here, index, *tokens, *factor, *more)


def grad_out_kernel(core_ref, *refs):
    slot_refs, (codes_ref, mine_ref, theirs_ref) = refs[:-3], refs[-3:]
    dims = (((0,), (0,)), ((), ()))
    codes = codes_ref[0]
    first = jnp.concatenate([s[0, 0] for s in slot_refs], axis=0)
    second = jnp.concatenate([s[0, 1] for s in slot_refs], axis=0)
    first = lax.dot_general(first, codes, dims, preferred_element_type=jnp.float32)
    second = lax.dot_general(second, codes, dims, preferred_element_type=jnp.float32)
    grad = jnp.where(low_lanes(first.shape), first, second)
    others, _, quarter, _ = mine_ref.shape
    first_core = core_ref[0] == 0
    for y in range(others):
        one = grad[2 * y * quarter : (2 * y + 1) * quarter]
        two = grad[(2 * y + 1) * quarter : (2 * y + 2) * quarter]
        mine_ref[y, 0] = jnp.where(first_core, one, two)
        theirs_ref[y, 0] = jnp.where(first_core, two, one)


def grad_out_call(core, slot_parts, codes, others, quarter):
    groups, slots, columns = codes.shape
    _, experts, _, width = slot_parts[0].shape
    pair = 2 * columns // experts
    return pl.pallas_call(
        grad_out_kernel,
        grid=(groups, experts // 2),
        in_specs=[pl.BlockSpec(memory_space=pltpu.SMEM)]
        + [
            pl.BlockSpec((1, 2, s.shape[2], width), lambda i, g: (i, g, 0, 0)) for s in slot_parts
        ]
        + [pl.BlockSpec((1, slots, pair), lambda i, g: (i, 0, g))],
        out_specs=[pl.BlockSpec((others, 1, quarter, pair), lambda i, g: (0, i, 0, g))] * 2,
        out_shape=[jax.ShapeDtypeStruct((others, groups, quarter, columns), jnp.float32)] * 2,
        compiler_params=pltpu.CompilerParams(vmem_limit_bytes=VMEM_LIMIT),
        cost_estimate=pl.CostEstimate(
            flops=groups * 4 * slots * width * columns,
            bytes_accessed=2 * groups * experts * slots * width + 4 * groups * width * columns,
            transcendentals=0,
        ),
        name="grad_out",
    )(core, *slot_parts, codes)


def turn(blocks, shift):
    count = blocks.shape[0]
    return lax.dynamic_slice_in_dim(jnp.concatenate([blocks, blocks], axis=0), shift, count, 0)


def over_dp(part):
    size = lax.axis_size("y")
    stack = [part]
    for k in range(1, size):
        stack.append(lax.ppermute(part, "y", [((i + k) % size, i) for i in range(size)]))
    mine = jnp.stack(stack)
    theirs = lax.ppermute(mine, "c", [(0, 1), (1, 0)])
    return mine, theirs


def around(mine):
    size = lax.axis_size("z")
    up = [(i, (i + 1) % size) for i in range(size)]
    down = [(i, (i - 1) % size) for i in range(size)]
    half = mine.shape[0] // 2
    groups = [[(0, mine)]]
    low = high = mine
    for k in range(1, size // 2):
        low = lax.ppermute(low, "z", up)
        high = lax.ppermute(high, "z", down)
        found = [(2 * (size - k), low), (2 * k, high)]
        if k < size // 2 - 1:
            groups[0] += found
        else:
            groups.append(found)
    k = size // 2
    low = lax.ppermute(low[:half], "z", up)
    high = lax.ppermute(high[half:], "z", down)
    groups.append([(2 * k, low), (2 * k + 1, high)])
    return groups


def local(
    route_experts,
    router_gate_weight,
    forget_mask,
    retain_mask,
    layer_output,
    frozen_output,
    control_vector,
    saved_hidden,
    adapter_in,
    adapter_out,
):
    experts, slot_count, _ = saved_hidden.shape
    tokens, features = layer_output.shape
    columns = adapter_in.shape[1]
    rank = columns // experts
    zs, xs = lax.axis_size("z"), lax.axis_size("x")
    dps = lax.axis_size("y") * lax.axis_size("c")
    blocks = zs * xs
    quarter = features // (dps * xs)
    width = features // xs

    others = lax.axis_size("y")
    twins = [(0, 1), (1, 0)]
    where = jnp.stack([lax.axis_index("c"), lax.axis_index("y")]).astype(jnp.int32)
    gathered_in = over_dp(adapter_in)

    cotangent = token_cotangent(
        layer_output, frozen_output, forget_mask, retain_mask, control_vector
    ).astype(jnp.bfloat16)
    parts = cotangent.reshape(tokens, dps, xs, quarter).transpose(2, 0, 1, 3)
    mine = lax.all_to_all(parts.reshape(xs * tokens, width), "x", 0, 0, tiled=True)
    groups = around(mine)

    token, weights = slot_tables(route_experts, router_gate_weight, blocks * experts)
    token = token.reshape(CAP, zs, 1, xs * experts).transpose(1, 2, 0, 3)
    token = jnp.broadcast_to(token, (zs, xs, CAP, xs * experts))
    weights = weights.reshape(CAP, zs, xs, experts).transpose(1, 2, 0, 3)
    table = jnp.concatenate([token, weights], axis=3)
    table = jnp.pad(
        table,
        ((0, 0), (0, 0), (0, PADC - CAP), (0, 128 - table.shape[3])),
        constant_values=-1.0,
    )
    table = lax.all_to_all(table.reshape(blocks * PADC, 128), ("z", "x"), 0, 0, tiled=True)
    table = table.reshape(blocks, PADC, 128)
    scale = table[:, :CAP, xs * experts : (xs + 1) * experts]
    scale = adapter_scale_factor * scale
    scale = jnp.broadcast_to(
        scale.reshape(slot_count, experts, 1), (slot_count, experts, rank)
    ).reshape(slot_count, columns)
    here = lax.axis_index("z")
    index = turn(table[:, :, : xs * experts].reshape(zs, xs, PADC, xs * experts), here)
    index = index.astype(jnp.int32)
    index = index.reshape(blocks // 2, 2, PADC, xs, experts)
    odd = jnp.arange(2, dtype=jnp.int32).reshape(1, 2, 1, 1, 1) * tokens
    index = jnp.where(index >= 0, index + odd, -1)
    index = index.transpose(3, 0, 4, 1, 2).reshape(xs, blocks // 2, experts * 2 * PADC)

    factor = lax.all_to_all(adapter_out, "x", 0, 0, tiled=True)
    factor = over_dp(factor.reshape(xs, quarter, columns))

    order = [start // 2 for group in groups for start, _ in group]
    order = list(dict.fromkeys(order))
    slot = jnp.arange(slot_count, dtype=jnp.int32)
    ahead = lax.rem(slot // (xs * CAP) - here + zs, zs)
    place = sum(jnp.where(ahead == o, n, 0) for n, o in enumerate(order))
    place = (place * xs + lax.rem(slot // CAP, xs)) * PADC + lax.rem(slot, CAP)
    pick = place[:, None] == jnp.arange(blocks * PADC, dtype=jnp.int32)[None, :]
    pick = pick.astype(jnp.bfloat16)

    codes = codes_call(where, saved_hidden, *gathered_in)
    codes = (lax.reduce_precision(codes, 8, 7) * scale).astype(jnp.bfloat16)
    codes = lax.dot_general(
        pick, codes, (((0,), (0,)), ((), ())), preferred_element_type=jnp.float32
    )
    codes = jnp.broadcast_to(codes.astype(jnp.bfloat16)[None], (xs, blocks * PADC, columns))
    codes = lax.all_to_all(codes, "x", 0, 0, tiled=True)

    step = 2 * PADC
    sizes = [sum(t.shape[0] for _, t in g) // (2 * tokens) * step for g in groups]
    places = [(sizes[0], 0), (sizes[1] + sizes[2], 0), (sizes[1] + sizes[2], sizes[1])]
    backs, slot_parts, part = [], [], None
    for n, group in enumerate(groups):
        starts, parts = [f[0] for f in group], [f[1] for f in group]
        into = part if places[n][1] else None
        part, slots = back_call(
            where, index, parts, starts, factor, experts, 2 * tokens, *places[n], into
        )
        slot_parts.append(slots)
        if n != 1:
            backs.append(lax.all_to_all(part, "x", 0, 0, tiled=True))
    out_mine, out_theirs = grad_out_call(where, slot_parts, codes, others, quarter)
    out_theirs = lax.ppermute(out_theirs, "c", twins)
    in_mine, in_theirs = grad_in_call(where, saved_hidden, pick, scale, backs, others)
    in_theirs = lax.ppermute(in_theirs, "c", twins)
    grad_out = (out_mine + out_theirs).astype(jnp.bfloat16)
    grad_out = grad_out.reshape(others * xs, quarter, columns)
    grad_out = lax.all_to_all(grad_out, ("y", "x"), 0, 0, tiled=True)
    grad_out = grad_out.reshape(others, xs * quarter, columns)
    grad_out = jnp.sum(grad_out.astype(jnp.float32), axis=0)
    grad_in = in_mine[0] + in_theirs[0]
    for k in range(1, others):
        piece = (in_mine[k] + in_theirs[k]).astype(jnp.bfloat16)
        piece = lax.ppermute(piece, "y", [(i, (i + k) % others) for i in range(others)])
        grad_in = grad_in + piece.astype(jnp.float32)
    return (grad_in, grad_out)


def solution(mesh):
    dps, blocks = mesh.devices.shape
    xs = 4 if blocks >= 32 else 2
    cores = 2
    fine = Mesh(
        mesh.devices.reshape(dps // cores, cores, blocks // xs, xs), ("y", "c", "z", "x")
    )
    dp, ep = ("y", "c"), ("z", "x")
    return jax.shard_map(
        local,
        mesh=fine,
        in_specs=(
            P(dp + ep, None),
            P(dp + ep, None),
            P(dp + ep),
            P(dp + ep),
            P(dp + ep, None),
            P(dp + ep, None),
            P(),
            P(dp + ep, None, None),
            P(dp, ep),
            P(dp, ep),
        ),
        out_specs=(P(dp, ep), P(dp, ep)),
        check_vma=False,
    )
```
